32 devices in a mesh: slab: 4 (over x, core), weight: 8 (over z, y).
Axes of the slice: x: 2, y: 2, z: 4, core: 2. Of those that a mesh axis runs over, the one named last changes fastest.
Arguments:
- tokens: bfloat16 [8192, 1536], P(('slab', 'weight')), may hold values from -6 to 6
- w_qkv: bfloat16 [1536, 384], P('weight', 'slab'), may hold values from -0.1875 to 0.1875
- w_proj: bfloat16 [128, 1536], P('slab', 'weight'), may hold values from -1.5 to 1.5
- grad_out: bfloat16 [8192, 1536], P(('slab', 'weight')), may hold values from -0.59765625 to 0.59765625
Outputs:
- mixed: bfloat16 [8192, 1536], P(('slab', 'weight'))
- grad_tokens: bfloat16 [8192, 1536], P(('slab', 'weight'))
- grad_qkv: float32 [1536, 384], P('weight', 'slab')
- grad_proj: float32 [128, 1536], P('slab', 'weight')
The draws below stay inside these ranges and needn't reach their ends.
All inputs are finite; a program needn't handle non-finite values.
Results may differ from the reference program's by a relative error of at most 0.013.
Values may be sent and summed in bfloat16 or wider, within the bound.
No kernel may reach another device: no remote copies, remote signals or barrier semaphores. Data moves between devices by JAX's collectives and lax.ppermute only.
A program may use at most 64 MiB of HBM per device.

```python
import jax
import jax.numpy as jnp
from jax import lax

D = 1536
HD = 128
HT = 2
TILE = 128
WT = 8
TOKENS = 8192
N_SLAB = 4


def draw_tokens(key, part):
    value_key = jax.random.fold_in(jax.random.fold_in(key, 3), 0)
    return jnp.clip(jax.random.normal(value_key, (TOKENS, D), jnp.float32), -6.0, 6.0).astype(jnp.bfloat16)


def level_of(key, extent, cuts, smallest, largest):
    loudness = 1.0
    for dim, shards_of in cuts:
        steps = jax.random.uniform(jax.random.fold_in(jax.random.fold_in(key, 6), dim), (shards_of,), jnp.float32, smallest / len(cuts), largest / len(cuts))
        loudness = loudness * jnp.repeat(jnp.exp(steps), extent[dim] // shards_of).reshape((-1,) + (1,) * (len(extent) - 1 - dim))
    return loudness


def noise(own_key, shape, deviation, bound, shards=(), kind=jnp.bfloat16):
    factor_of = level_of(own_key, shape, shards, -0.22, 0.18) if shards else 1.0
    array = jax.random.normal(own_key, shape, jnp.float32) * deviation * factor_of
    return jnp.minimum(jnp.maximum(array, -bound), bound).astype(kind)


def setup_inputs(seed: int = 0) -> dict:
    keys = jax.random.split(jax.random.key(seed), 5)
    return {
        "tokens": draw_tokens(jax.random.fold_in(keys[4], 71), 0),
        "w_qkv": noise(keys[1], (D, 3 * HD), (1.3 * D ** -0.5), 0.1875, ((0, 8), (1, 4))),
        "w_proj": noise(keys[2], (HD, D), (3 * HD ** -0.5), 1.5, ((0, 4), (1, 8))),
        "grad_out": noise(keys[3], (TOKENS, D), 0.1, 0.59765625, ((0, 32),)),
    }


def rounded_copy(values):
    return lax.optimization_barrier(values.astype(jnp.bfloat16)).astype(jnp.float32)


def reference(tokens, w_qkv, w_proj, grad_out):
    inverse_root = HD ** -0.5
    grid_shape = (N_SLAB, WT, HT, TILE)
    projected = jnp.dot(tokens, w_qkv, preferred_element_type=jnp.float32).astype(jnp.bfloat16)
    queries = projected[:, :HD].reshape(grid_shape + (HD,))
    key_value = jnp.pad(projected[:, HD:].reshape(grid_shape + (2 * HD,)), ((1, 1), (1, 1), (1, 1), (0, 0), (0, 0)))
    present = jnp.pad(jnp.ones((N_SLAB, WT, HT), jnp.float32), 1)
    grad_attended = jnp.dot(grad_out, w_proj.T, preferred_element_type=jnp.float32).astype(jnp.bfloat16)
    grad_attended = grad_attended.reshape(grid_shape + (HD,))
    anchor = jnp.zeros((), jnp.int32)

    def slab_step(pair_grads, slab_index):
        query_full = lax.dynamic_index_in_dim(queries, slab_index, 0, keepdims=False).astype(jnp.float32)
        cotangent = lax.dynamic_index_in_dim(grad_attended, slab_index, 0, keepdims=False).astype(jnp.float32)
        corners = []
        blocks = []
        presence = []
        for window_entry in range(27):
            time_step = window_entry // 9 - 1
            first_step = (window_entry // 3) % 3 - 1
            second_step = window_entry % 3 - 1
            corner = ((slab_index + 1 + time_step).astype(jnp.int32), jnp.asarray(1 + first_step, jnp.int32), jnp.asarray(1 + second_step, jnp.int32))
            corners.append(corner)
            blocks.append(lax.dynamic_slice(key_value, corner + (anchor, anchor), (1, WT, HT, TILE, 2 * HD))[0])
            presence.append(lax.dynamic_slice(present, corner, (1, WT, HT))[0])
        window = jnp.stack(blocks, axis=2).astype(jnp.float32)
        inside = jnp.stack(presence, axis=2) > 0.5
        window_keys = window[..., :HD]
        window_values = window[..., HD:]
        scores = jnp.einsum("hwqd,hwjkd->hwqjk", query_full, window_keys) * inverse_root
        scores = jnp.where(inside[:, :, None, :, None], scores, -jnp.inf)
        highest = jnp.max(scores, axis=(3, 4), keepdims=True)
        log_total = highest + jnp.log(jnp.sum(jnp.exp(scores - highest), axis=(3, 4), keepdims=True))
        weights = jnp.exp(scores - log_total)
        weights_half = rounded_copy(weights)
        attended = jnp.einsum("hwqjk,hwjkd->hwqd", weights_half, window_values).astype(jnp.bfloat16)
        row_delta = jnp.sum(cotangent * attended.astype(jnp.float32), axis=-1)
        grad_weights = jnp.einsum("hwqd,hwjkd->hwqjk", cotangent, window_values)
        grad_scores = rounded_copy(weights * (grad_weights - row_delta[..., None, None]))
        grad_queries = (jnp.einsum("hwqjk,hwjkd->hwqd", grad_scores, window_keys) * inverse_root).astype(jnp.bfloat16)
        grad_keys = jnp.einsum("hwqjk,hwqd->hwjkd", grad_scores, query_full) * inverse_root
        grad_values = jnp.einsum("hwqjk,hwqd->hwjkd", weights_half, cotangent)
        key_parts = rounded_copy(jnp.concatenate([grad_keys, grad_values], axis=-1))
        for window_entry in range(27):
            corner = corners[window_entry] + (anchor, anchor)
            current = lax.dynamic_slice(pair_grads, corner, (1, WT, HT, TILE, 2 * HD))
            pair_grads = lax.dynamic_update_slice(pair_grads, current + key_parts[:, :, window_entry][None], corner)
        return pair_grads, (attended, grad_queries)

    pair_grads, outputs = lax.scan(slab_step, jnp.zeros(key_value.shape, jnp.float32), jnp.arange(N_SLAB, dtype=jnp.int32))
    attended = outputs[0].reshape(TOKENS, HD)
    grad_queries = outputs[1].reshape(TOKENS, HD)
    mixed = jnp.dot(attended, w_proj, preferred_element_type=jnp.float32).astype(jnp.bfloat16)
    grad_pairs = pair_grads[1:-1, 1:-1, 1:-1].astype(jnp.bfloat16).reshape(TOKENS, 2 * HD)
    grad_rows = jnp.concatenate([grad_queries, grad_pairs], axis=1)
    grad_tokens = jnp.dot(grad_rows, w_qkv.T, preferred_element_type=jnp.float32).astype(jnp.bfloat16)
    group_rows = HT * TILE
    group_count = TOKENS // group_rows

    def group_step(totals, pieces):
        token_group, rows_group, cotangent_group, attended_group = pieces
        first_part = rounded_copy(jnp.dot(token_group.T, rows_group, preferred_element_type=jnp.float32))
        second_part = rounded_copy(jnp.dot(cotangent_group.T, attended_group, preferred_element_type=jnp.float32))
        return (totals[0] + first_part, totals[1] + second_part), None

    starting = (jnp.zeros((D, 3 * HD), jnp.float32), jnp.zeros((D, HD), jnp.float32))
    pieces = (tokens.reshape(group_count, group_rows, D), grad_rows.reshape(group_count, group_rows, 3 * HD),
              grad_out.reshape(group_count, group_rows, D), attended.reshape(group_count, group_rows, HD))
    totals, ignored = lax.scan(group_step, starting, pieces)
    return mixed, grad_tokens, totals[0], totals[1].T
```

```python
import functools

import jax
import jax.numpy as jnp
from jax import lax
from jax.experimental import pallas as pl
from jax.experimental.pallas import tpu as pltpu
from jax.sharding import PartitionSpec as P

HD = 128
AXES = ("slab", "weight")
BF = jnp.bfloat16
F32 = jnp.float32
VMEM = pl.BlockSpec(memory_space=pltpu.VMEM)
SMEM = pl.BlockSpec(memory_space=pltpu.SMEM)


def bits_of(size):
    return size.bit_length() - 1


def exchange_steps(slabs, weights):
    steps = [("weight", bit) for bit in reversed(range(1, bits_of(weights)))]
    steps += [("slab", bit) for bit in reversed(range(2, bits_of(slabs)))]
    return steps + [("first", 0), ("second", 0)]


def step_mask(step, odd):
    kind, bit = step
    if kind == "weight":
        return 0, 1 << bit
    if kind == "slab":
        return 1 << bit, 0
    along_slab = 1 - odd if kind == "first" else odd
    return 2 * along_slab, 1 - along_slab


def block_owner(block, steps, slab, weight, odd):
    for place, step in enumerate(steps):
        if block >> place & 1:
            slab_mask, weight_mask = step_mask(step, odd)
            slab, weight = slab ^ slab_mask, weight ^ weight_mask
    return slab, weight


def step_pairs(step, slabs, weights):
    pairs = []
    for s in range(slabs):
        for w in range(weights):
            slab_mask, weight_mask = step_mask(step, s & 1)
            pairs.append((s * weights + w, (s ^ slab_mask) * weights + (w ^ weight_mask)))
    return pairs


def core_pairs(slabs, weights):
    return [(s * weights + w, (s ^ 1) * weights + w) for s in range(slabs) for w in range(weights)]


def paired(index, size, odd):
    other = ((index + odd) ^ 1) - odd
    return other if 0 <= other < size else None


def slab_pairs(odd, slabs, weights):
    return [
        (s * weights + w, paired(s, slabs, odd) * weights + w)
        for s in range(slabs)
        for w in range(weights)
        if paired(s, slabs, odd) is not None
    ]


def weight_pairs(odd, slabs, weights):
    return [
        (s * weights + w, s * weights + paired(w, weights, odd))
        for s in range(slabs)
        for w in range(weights)
        if paired(w, weights, odd) is not None
    ]


def dot(a, b, dims=((1,), (0,))):
    return lax.dot_general(a, b, (dims, ((), ())), preferred_element_type=F32)


def pack_kernel(qkv_ref, proj_ref, out_ref):
    out_ref[0] = jnp.concatenate([qkv_ref[...], proj_ref[...].T], axis=1)


def project_kernel(steps, split, index, own, got, tokens, grad_out, q_ref, kv_ref, co_ref, full):
    slab, weight = index[0], index[1]
    odd = slab & 1
    rows = own.shape[1]
    for half, (source, where, parity) in enumerate(((own, slab, odd), (got, slab ^ 1, 1 - odd))):
        for block in range(own.shape[0]):
            s, w = block_owner(block, steps, where, weight, parity)
            full[s, pl.ds(pl.multiple_of(w * rows, rows), rows), :] = source[block]
    slabs = full.shape[0]
    projected = [dot(tokens[...], full[s])[:, :split].astype(BF) for s in range(slabs)]
    cotangent = [dot(grad_out[...], full[s])[:, split:].astype(BF) for s in range(slabs)]
    projected = jnp.concatenate(projected, axis=1)
    q_ref[...] = projected[:, :HD]
    kv_ref[...] = projected[:, HD:]
    co_ref[...] = jnp.concatenate(cotangent, axis=1)


def attention_kernel(
    sizes, index, q_ref, co_ref, own, even, odd, slab_even, slab_odd,
    att_ref, dq_ref, parts_own, parts_even, parts_odd, scores,
):
    slab, weight = index[0], index[1]
    slabs, weights = sizes
    root = HD ** (-0.5)
    slab_inside = (slab > 0) & (slab < slabs - 1)
    weight_inside = (weight > 0) & (weight < weights - 1)
    blocks = [own, even, odd]
    blocks += [slab_even.at[i] for i in range(3)] + [slab_odd.at[i] for i in range(3)]
    outs = [parts.at[i] for parts in (parts_own, parts_even, parts_odd) for i in range(3)]
    query, cotangent = q_ref[...], co_ref[...]
    highest = None
    for j, block in enumerate(blocks):
        part = dot(query, block[:, :HD], ((1,), (1,))) * root
        present = None
        if j % 3 == 2:
            present = weight_inside
        if j >= 6:
            present = slab_inside if present is None else present & slab_inside
        if present is not None:
            part = part + jnp.where(present, 0.0, -jnp.inf)
        scores[j] = part
        highest = part if highest is None else jnp.maximum(highest, part)
    highest = jnp.max(highest, axis=1, keepdims=True)
    total = None
    for j in range(9):
        part = jnp.exp(scores[j] - highest)
        scores[j] = part
        total = part if total is None else total + part
    scale = 1.0 / jnp.sum(total, axis=1, keepdims=True)
    attended = None
    for j, block in enumerate(blocks):
        weighted = dot((scores[j] * scale).astype(BF), block[:, HD:])
        attended = weighted if attended is None else attended + weighted
    attended = attended.astype(BF)
    att_ref[...] = attended
    delta = jnp.sum(cotangent.astype(F32) * attended.astype(F32), axis=1, keepdims=True)
    grad_query = None
    for j, (block, out) in enumerate(zip(blocks, outs)):
        grad = dot(cotangent, block[:, HD:], ((1,), (1,)))
        part = scores[j] * scale
        grad = (part * (grad - delta)).astype(BF)
        step = dot(grad, block[:, :HD])
        grad_query = step if grad_query is None else grad_query + step
        out[:, :HD] = (dot(grad, query, ((0,), (0,))) * root).astype(BF)
        out[:, HD:] = dot(part.astype(BF), cotangent, ((0,), (0,))).astype(BF)
    dq_ref[...] = (grad_query * root).astype(BF)


def mixed_kernel(split, att_ref, full, out_ref):
    slabs = full.shape[0]
    width = HD // slabs
    attended = att_ref[...]
    zeros = jnp.zeros((attended.shape[0], split), BF)
    total = None
    for s in range(slabs):
        part = jnp.concatenate([zeros, attended[:, s * width : (s + 1) * width]], axis=1)
        part = dot(part, full[s], ((1,), (1,)))
        total = part if total is None else total + part
    out_ref[...] = total.astype(BF)


def weight_grads_kernel(
    steps, slabs, split, index, tokens, grad_out, dq, own, even, odd, att_ref,
    rows_ref, keep, send, full,
):
    slab, weight = index[0], index[1]
    parity = slab & 1
    pairs = own[...] + even[...].astype(F32) + odd[...].astype(F32)
    rows = jnp.concatenate([dq[...], pairs.astype(BF)], axis=1)
    rows_ref[...] = rows
    attended = att_ref[...]
    width = HD // slabs
    count = rows.shape[0]
    left_zeros = jnp.zeros((count, width), BF)
    right_zeros = jnp.zeros((count, split), BF)
    left, right = [], []
    for s in range(slabs):
        left += [rows[:, s * split : (s + 1) * split], left_zeros]
        right += [right_zeros, attended[:, s * width : (s + 1) * width]]
    grads = dot(tokens[...], jnp.concatenate(left, axis=1), ((0,), (0,)))
    grads = grads + dot(grad_out[...], jnp.concatenate(right, axis=1), ((0,), (0,)))
    lanes = split + width
    for s in range(slabs):
        full[s] = grads[:, s * lanes : (s + 1) * lanes].astype(BF)
    size = keep.shape[1]
    for target, where, odd_core in ((send, slab ^ 1, 1 - parity), (keep, slab, parity)):
        for block in range(keep.shape[0]):
            s, w = block_owner(block, steps, where, weight, odd_core)
            target[block] = full[s, pl.ds(pl.multiple_of(w * size, size), size), :]


def grad_tokens_kernel(split, rows_ref, full, out_ref):
    slabs = full.shape[0]
    rows = rows_ref[...]
    zeros = jnp.zeros((rows.shape[0], HD // slabs), BF)
    total = None
    for s in range(slabs):
        part = jnp.concatenate([rows[:, s * split : (s + 1) * split], zeros], axis=1)
        part = dot(part, full[s], ((1,), (1,)))
        total = part if total is None else total + part
    out_ref[...] = total.astype(BF)


def unpack_kernel(split, keep, got, qkv_ref, proj_ref):
    total = keep[0] + got[0].astype(F32)
    qkv_ref[...] = total[:, :split]
    proj_ref[...] = total[:, split:].T


def call(kernel, outs, args, scratch=(), scalars=0):
    shapes = [jax.ShapeDtypeStruct(shape, kind) for shape, kind in outs]
    return pl.pallas_call(
        kernel,
        out_shape=shapes,
        in_specs=[SMEM] * scalars + [VMEM] * (len(args) - scalars),
        out_specs=[VMEM] * len(outs),
        scratch_shapes=list(scratch),
    )(*args)


def local(slabs, weights, tokens, w_qkv, w_proj, grad_out):
    steps = exchange_steps(slabs, weights)
    index = jnp.stack([lax.axis_index("slab"), lax.axis_index("weight")]).astype(jnp.int32)
    count, features = tokens.shape
    rows, split = w_qkv.shape
    lanes = split + HD // slabs

    def swap(values, pairs):
        return lax.ppermute(values, AXES, pairs)

    (held,) = call(pack_kernel, [((1, rows, lanes), BF)], [w_qkv, w_proj])
    for step in steps:
        held = jnp.concatenate([held, swap(held, step_pairs(step, slabs, weights))], axis=0)
    got = swap(held, core_pairs(slabs, weights))
    query, key_value, cotangent, full = call(
        functools.partial(project_kernel, steps, split),
        [((count, HD), BF), ((count, 2 * HD), BF), ((count, HD), BF), ((slabs, features, lanes), BF)],
        [index, held, got, tokens, grad_out],
        scalars=1,
    )

    weight_even, weight_odd = (weight_pairs(odd, slabs, weights) for odd in (0, 1))
    slab_even, slab_odd = (slab_pairs(odd, slabs, weights) for odd in (0, 1))
    even, odd = swap(key_value, weight_even), swap(key_value, weight_odd)
    columns = jnp.stack([key_value, even, odd])
    across_even, across_odd = swap(columns, slab_even), swap(columns, slab_odd)
    pair = (3, count, 2 * HD)
    attended, grad_query, parts_own, parts_even, parts_odd = call(
        functools.partial(attention_kernel, (slabs, weights)),
        [((count, HD), BF), ((count, HD), BF), (pair, BF), (pair, BF), (pair, BF)],
        [index, query, cotangent, key_value, even, odd, across_even, across_odd],
        scratch=[pltpu.VMEM((9, count, count), F32)],
        scalars=1,
    )
    parts_even, parts_odd = swap(parts_even, slab_even), swap(parts_odd, slab_odd)
    (mixed,) = call(
        functools.partial(mixed_kernel, split), [((count, features), BF)], [attended, full]
    )

    def summed(column):
        return (
            parts_own[column].astype(F32)
            + parts_even[column].astype(F32)
            + parts_odd[column].astype(F32)
        )

    even = swap(summed(1).astype(BF), weight_even)
    odd = swap(summed(2).astype(BF), weight_odd)
    half = (1 << len(steps), rows, lanes)
    grad_rows, keep, send = call(
        functools.partial(weight_grads_kernel, steps, slabs, split),
        [((count, 3 * HD), BF), (half, BF), (half, BF)],
        [index, tokens, grad_out, grad_query, summed(0), even, odd, attended],
        scratch=[pltpu.VMEM((slabs, features, lanes), BF)],
        scalars=1,
    )
    got = swap(send, core_pairs(slabs, weights))
    (grad_tokens,) = call(
        functools.partial(grad_tokens_kernel, split), [((count, features), BF)], [grad_rows, full]
    )
    for step in reversed(steps):
        near = keep.shape[0] // 2
        send = (keep[near:].astype(F32) + got[near:].astype(F32)).astype(BF)
        keep = keep[:near].astype(F32) + got[:near].astype(F32)
        got = swap(send, step_pairs(step, slabs, weights))
    grad_qkv, grad_proj = call(
        functools.partial(unpack_kernel, split),
        [((rows, split), F32), ((HD // slabs, rows), F32)],
        [keep, got],
    )
    return mixed, grad_tokens, grad_qkv, grad_proj


def solution(mesh):
    in_specs = (
        P(AXES, None),
        P("weight", "slab"),
        P("slab", "weight"),
        P(AXES, None),
    )
    out_specs = (
        P(AXES, None),
        P(AXES, None),
        P("weight", "slab"),
        P("slab", "weight"),
    )
    body = functools.partial(local, mesh.shape["slab"], mesh.shape["weight"])
    return jax.shard_map(body, mesh=mesh, in_specs=in_specs, out_specs=out_specs, check_vma=False)
```

```python
import functools

import jax
import jax.numpy as jnp
from jax import lax
from jax.experimental import pallas as pl
from jax.experimental.pallas import tpu as pltpu
from jax.sharding import PartitionSpec as P

HD = 128
AXES = ("slab", "weight")
BF = jnp.bfloat16
F32 = jnp.float32
VMEM = pl.BlockSpec(memory_space=pltpu.VMEM)
SMEM = pl.BlockSpec(memory_space=pltpu.SMEM)


def bits_of(size):
    return size.bit_length() - 1


def exchange_steps(slabs, weights):
    steps = [("weight", bit) for bit in reversed(range(1, bits_of(weights)))]
    steps += [("slab", bit) for bit in reversed(range(2, bits_of(slabs)))]
    return steps + [("first", 0), ("second", 0)]


def step_mask(step, odd):
    kind, bit = step
    if kind == "weight":
        return 0, 1 << bit
    if kind == "slab":
        return 1 << bit, 0
    along_slab = 1 - odd if kind == "first" else odd
    return 2 * along_slab, 1 - along_slab


def block_owner(block, steps, slab, weight, odd):
    for place, step in enumerate(steps):
        if block >> place & 1:
            slab_mask, weight_mask = step_mask(step, odd)
            slab, weight = slab ^ slab_mask, weight ^ weight_mask
    return slab, weight


def step_pairs(step, slabs, weights):
    pairs = []
    for s in range(slabs):
        for w in range(weights):
            slab_mask, weight_mask = step_mask(step, s & 1)
            pairs.append((s * weights + w, (s ^ slab_mask) * weights + (w ^ weight_mask)))
    return pairs


def core_pairs(slabs, weights):
    return [(s * weights + w, (s ^ 1) * weights + w) for s in range(slabs) for w in range(weights)]


def paired(index, size, odd):
    other = ((index + odd) ^ 1) - odd
    return other if 0 <= other < size else None


def slab_pairs(odd, slabs, weights):
    return [
        (s * weights + w, paired(s, slabs, odd) * weights + w)
        for s in range(slabs)
        for w in range(weights)
        if paired(s, slabs, odd) is not None
    ]


def weight_pairs(odd, slabs, weights):
    return [
        (s * weights + w, s * weights + paired(w, weights, odd))
        for s in range(slabs)
        for w in range(weights)
        if paired(w, weights, odd) is not None
    ]


def dot(a, b, dims=((1,), (0,))):
    return lax.dot_general(a, b, (dims, ((), ())), preferred_element_type=F32)


def pack_kernel(qkv_ref, proj_ref, out_ref):
    out_ref[0] = jnp.concatenate([qkv_ref[...], proj_ref[...].T], axis=1)


def project_kernel(steps, split, index, own, got, tokens, grad_out, q_ref, kv_ref, co_ref, full):
    slab, weight = index[0], index[1]
    odd = slab & 1
    rows = own.shape[1]
    for half, (source, where, parity) in enumerate(((own, slab, odd), (got, slab ^ 1, 1 - odd))):
        for block in range(own.shape[0]):
            s, w = block_owner(block, steps, where, weight, parity)
            full[s, pl.ds(pl.multiple_of(w * rows, rows), rows), :] = source[block]
    slabs = full.shape[0]
    projected = [dot(tokens[...], full[s])[:, :split].astype(BF) for s in range(slabs)]
    cotangent = [dot(grad_out[...], full[s])[:, split:].astype(BF) for s in range(slabs)]
    projected = jnp.concatenate(projected, axis=1)
    q_ref[...] = projected[:, :HD]
    kv_ref[...] = projected[:, HD:]
    co_ref[...] = jnp.concatenate(cotangent, axis=1)


def attention_kernel(
    sizes, index, q_ref, co_ref, own, even, odd, slab_even, slab_odd,
    att_ref, dq_ref, parts_own, parts_even, parts_odd, scores,
):
    slab, weight = index[0], index[1]
    slabs, weights = sizes
    root = HD ** (-0.5)
    slab_inside = (slab > 0) & (slab < slabs - 1)
    weight_inside = (weight > 0) & (weight < weights - 1)
    blocks = [own, even, odd]
    blocks += [slab_even.at[i] for i in range(3)] + [slab_odd.at[i] for i in range(3)]
    outs = [parts.at[i] for parts in (parts_own, parts_even, parts_odd) for i in range(3)]
    query, cotangent = q_ref[...], co_ref[...]
    highest = None
    for j, block in enumerate(blocks):
        part = dot(query, block[:, :HD], ((1,), (1,))) * root
        present = None
        if j % 3 == 2:
            present = weight_inside
        if j >= 6:
            present = slab_inside if present is None else present & slab_inside
        if present is not None:
            part = part + jnp.where(present, 0.0, -jnp.inf)
        scores[j] = part
        highest = part if highest is None else jnp.maximum(highest, part)
    highest = jnp.max(highest, axis=1, keepdims=True)
    total = None
    for j in range(9):
        part = jnp.exp(scores[j] - highest)
        scores[j] = part
        total = part if total is None else total + part
    scale = 1.0 / jnp.sum(total, axis=1, keepdims=True)
    attended = None
    for j, block in enumerate(blocks):
        weighted = dot((scores[j] * scale).astype(BF), block[:, HD:])
        attended = weighted if attended is None else attended + weighted
    attended = attended.astype(BF)
    att_ref[...] = attended
    delta = jnp.sum(cotangent.astype(F32) * attended.astype(F32), axis=1, keepdims=True)
    grad_query = None
    for j, (block, out) in enumerate(zip(blocks, outs)):
        grad = dot(cotangent, block[:, HD:], ((1,), (1,)))
        part = scores[j] * scale
        grad = (part * (grad - delta)).astype(BF)
        step = dot(grad, block[:, :HD])
        grad_query = step if grad_query is None else grad_query + step
        out[:, :HD] = (dot(grad, query, ((0,), (0,))) * root).astype(BF)
        out[:, HD:] = dot(part.astype(BF), cotangent, ((0,), (0,))).astype(BF)
    dq_ref[...] = (grad_query * root).astype(BF)


def mixed_kernel(split, att_ref, full, out_ref):
    slabs = full.shape[0]
    width = HD // slabs
    attended = att_ref[...]
    zeros = jnp.zeros((attended.shape[0], split), BF)
    total = None
    for s in range(slabs):
        part = jnp.concatenate([zeros, attended[:, s * width : (s + 1) * width]], axis=1)
        part = dot(part, full[s], ((1,), (1,)))
        total = part if total is None else total + part
    out_ref[...] = total.astype(BF)


def weight_grads_kernel(
    steps, slabs, split, index, tokens, grad_out, dq, own, even, odd, att_ref,
    rows_ref, keep, send, full,
):
    slab, weight = index[0], index[1]
    parity = slab & 1
    pairs = own[...] + even[...].astype(F32) + odd[...].astype(F32)
    rows = jnp.concatenate([dq[...], pairs.astype(BF)], axis=1)
    rows_ref[...] = rows
    attended = att_ref[...]
    width = HD // slabs
    count = rows.shape[0]
    left_zeros = jnp.zeros((count, width), BF)
    right_zeros = jnp.zeros((count, split), BF)
    left, right = [], []
    for s in range(slabs):
        left += [rows[:, s * split : (s + 1) * split], left_zeros]
        right += [right_zeros, attended[:, s * width : (s + 1) * width]]
    grads = dot(tokens[...], jnp.concatenate(left, axis=1), ((0,), (0,)))
    grads = grads + dot(grad_out[...], jnp.concatenate(right, axis=1), ((0,), (0,)))
    lanes = split + width
    for s in range(slabs):
        full[s] = grads[:, s * lanes : (s + 1) * lanes].astype(BF)
    size = keep.shape[1]
    for target, where, odd_core in ((send, slab ^ 1, 1 - parity), (keep, slab, parity)):
        for block in range(keep.shape[0]):
            s, w = block_owner(block, steps, where, weight, odd_core)
            target[block] = full[s, pl.ds(pl.multiple_of(w * size, size), size), :]


def grad_tokens_kernel(split, rows_ref, full, out_ref):
    slabs = full.shape[0]
    rows = rows_ref[...]
    zeros = jnp.zeros((rows.shape[0], HD // slabs), BF)
    total = None
    for s in range(slabs):
        part = jnp.concatenate([rows[:, s * split : (s + 1) * split], zeros], axis=1)
        part = dot(part, full[s], ((1,), (1,)))
        total = part if total is None else total + part
    out_ref[...] = total.astype(BF)


def unpack_kernel(split, keep, got, qkv_ref, proj_ref):
    total = keep[0] + got[0].astype(F32)
    qkv_ref[...] = total[:, :split]
    proj_ref[...] = total[:, split:].T


def call(kernel, outs, args, scratch=(), scalars=0, final=False):
    make = jax.ShapeDtypeStruct if final else pltpu.VMEM
    args = [
        value if i < scalars else pltpu.with_memory_space_constraint(value, pltpu.VMEM)
        for i, value in enumerate(args)
    ]
    return pl.pallas_call(
        kernel,
        out_shape=[make(shape, kind) for shape, kind in outs],
        in_specs=[SMEM] * scalars + [VMEM] * (len(args) - scalars),
        out_specs=[VMEM] * len(outs),
        scratch_shapes=list(scratch),
        compiler_params=pltpu.CompilerParams(vmem_limit_bytes=32 << 20),
    )(*args)


def local(slabs, weights, tokens, w_qkv, w_proj, grad_out):
    steps = exchange_steps(slabs, weights)
    index = jnp.stack([lax.axis_index("slab"), lax.axis_index("weight")]).astype(jnp.int32)
    count, features = tokens.shape
    rows, split = w_qkv.shape
    lanes = split + HD // slabs

    def swap(values, pairs):
        return lax.ppermute(values, AXES, pairs)

    (held,) = call(pack_kernel, [((1, rows, lanes), BF)], [w_qkv, w_proj])
    for step in steps:
        held = jnp.concatenate([held, swap(held, step_pairs(step, slabs, weights))], axis=0)
    got = swap(held, core_pairs(slabs, weights))
    query, key_value, cotangent, full = call(
        functools.partial(project_kernel, steps, split),
        [((count, HD), BF), ((count, 2 * HD), BF), ((count, HD), BF), ((slabs, features, lanes), BF)],
        [index, held, got, tokens, grad_out],
        scalars=1,
    )

    weight_even, weight_odd = (weight_pairs(odd, slabs, weights) for odd in (0, 1))
    slab_even, slab_odd = (slab_pairs(odd, slabs, weights) for odd in (0, 1))
    even, odd = swap(key_value, weight_even), swap(key_value, weight_odd)
    columns = jnp.stack([key_value, even, odd])
    across_even, across_odd = swap(columns, slab_even), swap(columns, slab_odd)
    pair = (3, count, 2 * HD)
    attended, grad_query, parts_own, parts_even, parts_odd = call(
        functools.partial(attention_kernel, (slabs, weights)),
        [((count, HD), BF), ((count, HD), BF), (pair, BF), (pair, BF), (pair, BF)],
        [index, query, cotangent, key_value, even, odd, across_even, across_odd],
        scratch=[pltpu.VMEM((9, count, count), F32)],
        scalars=1,
    )
    parts_even, parts_odd = swap(parts_even, slab_even), swap(parts_odd, slab_odd)
    (mixed,) = call(
        functools.partial(mixed_kernel, split),
        [((count, features), BF)],
        [attended, full],
        final=True,
    )
    parts_even, parts_odd, mixed = lax.optimization_barrier((parts_even, parts_odd, mixed))

    def summed(column):
        return (
            parts_own[column].astype(F32)
            + parts_even[column].astype(F32)
            + parts_odd[column].astype(F32)
        )

    even = swap(summed(1).astype(BF), weight_even)
    odd = swap(summed(2).astype(BF), weight_odd)
    half = (1 << len(steps), rows, lanes)
    grad_rows, keep, send = call(
        functools.partial(weight_grads_kernel, steps, slabs, split),
        [((count, 3 * HD), BF), (half, BF), (half, BF)],
        [index, tokens, grad_out, grad_query, summed(0), even, odd, attended],
        scratch=[pltpu.VMEM((slabs, features, lanes), BF)],
        scalars=1,
    )
    got = swap(send, core_pairs(slabs, weights))
    for step in reversed(steps):
        near = keep.shape[0] // 2
        send = (keep[near:].astype(F32) + got[near:].astype(F32)).astype(BF)
        keep = keep[:near].astype(F32) + got[:near].astype(F32)
        got = swap(send, step_pairs(step, slabs, weights))
        if step == steps[-1]:
            (grad_tokens,) = call(
                functools.partial(grad_tokens_kernel, split),
                [((count, features), BF)],
                [grad_rows, full],
                final=True,
            )
            got, grad_tokens = lax.optimization_barrier((got, grad_tokens))
    grad_qkv, grad_proj = call(
        functools.partial(unpack_kernel, split),
        [((rows, split), F32), ((HD // slabs, rows), F32)],
        [keep, got],
        final=True,
    )
    return mixed, grad_tokens, grad_qkv, grad_proj


def solution(mesh):
    in_specs = (
        P(AXES, None),
        P("weight", "slab"),
        P("slab", "weight"),
        P(AXES, None),
    )
    out_specs = (
        P(AXES, None),
        P(AXES, None),
        P("weight", "slab"),
        P("slab", "weight"),
    )
    body = functools.partial(local, mesh.shape["slab"], mesh.shape["weight"])
    return jax.shard_map(body, mesh=mesh, in_specs=in_specs, out_specs=out_specs, check_vma=False)
```

```python
import functools
import math

import jax
import jax.numpy as jnp
from jax import lax
from jax.experimental import pallas as pl
from jax.experimental.pallas import tpu as pltpu
from jax.sharding import PartitionSpec as P

HD = 128
AXES = ("slab", "weight")
BF = jnp.bfloat16
F32 = jnp.float32
VMEM = pl.BlockSpec(memory_space=pltpu.VMEM)
SMEM = pl.BlockSpec(memory_space=pltpu.SMEM)


def bits_of(size):
    return size.bit_length() - 1


def exchange_steps(slabs, weights):
    steps = [((0, 1 << bit),) * 2 for bit in reversed(range(2, bits_of(weights)))]
    steps += [((1 << bit, 0),) * 2 for bit in reversed(range(2, bits_of(slabs)))]
    first, second, third = (2, 0), (0, 1), (0, 2)
    return steps + [(first, second), (second, third), (third, first)]


def block_owner(block, steps, slab, weight, odd):
    for place, (even_mask, odd_mask) in enumerate(steps):
        if block >> place & 1:
            slab = slab ^ (even_mask[0] * (1 - odd) + odd_mask[0] * odd)
            weight = weight ^ (even_mask[1] * (1 - odd) + odd_mask[1] * odd)
    return slab, weight


def step_pairs(step, slabs, weights):
    pairs = []
    for s in range(slabs):
        for w in range(weights):
            slab_mask, weight_mask = step[s & 1]
            pairs.append((s * weights + w, (s ^ slab_mask) * weights + (w ^ weight_mask)))
    return pairs


def core_pairs(slabs, weights):
    return [(s * weights + w, (s ^ 1) * weights + w) for s in range(slabs) for w in range(weights)]


def paired(index, size, odd):
    other = ((index + odd) ^ 1) - odd
    return other if 0 <= other < size else None


def slab_pairs(odd, slabs, weights):
    return [
        (s * weights + w, paired(s, slabs, odd) * weights + w)
        for s in range(slabs)
        for w in range(weights)
        if paired(s, slabs, odd) is not None
    ]


def weight_pairs(odd, slabs, weights):
    return [
        (s * weights + w, s * weights + paired(w, weights, odd))
        for s in range(slabs)
        for w in range(weights)
        if paired(w, weights, odd) is not None
    ]


def dot(a, b, dims=((1,), (0,))):
    return lax.dot_general(a, b, (dims, ((), ())), preferred_element_type=F32)


def pack_kernel(qkv_hbm, proj_hbm, out_ref, qkv_ref, proj_ref, arrived):
    first = pltpu.make_async_copy(qkv_hbm, qkv_ref, arrived.at[0])
    second = pltpu.make_async_copy(proj_hbm, proj_ref, arrived.at[1])
    first.start()
    second.start()
    first.wait()
    second.wait()
    out_ref[0] = jnp.concatenate([qkv_ref[...], proj_ref[...].T], axis=1)


def turn_kernel(tokens, grad_out, out_ref):
    count = tokens.shape[0]
    out_ref[:, :count] = tokens[...].T
    out_ref[:, count:] = grad_out[...].T


def project_kernel(steps, split, index, own, got, tokens, grad_out, q_ref, kv_ref, co_ref, full):
    slab, weight = index[0], index[1]
    odd = slab & 1
    rows = own.shape[1]
    for half, (source, where, parity) in enumerate(((own, slab, odd), (got, slab ^ 1, 1 - odd))):
        for block in range(own.shape[0]):
            s, w = block_owner(block, steps, where, weight, parity)
            full[s, pl.ds(pl.multiple_of(w * rows, rows), rows), :] = source[block]
    slabs = full.shape[0]
    projected = [dot(tokens[...], full[s])[:, :split].astype(BF) for s in range(slabs)]
    cotangent = [dot(grad_out[...], full[s])[:, split:].astype(BF) for s in range(slabs)]
    projected = jnp.concatenate(projected, axis=1)
    q_ref[...] = projected[:, :HD]
    kv_ref[...] = projected[:, HD:]
    co_ref[...] = jnp.concatenate(cotangent, axis=1)


def attention_kernel(
    sizes, index, q_ref, co_ref, own, even, odd, slab_even, slab_odd,
    att_ref, dq_ref, parts_own, parts_even, parts_odd, scores, halves,
):
    slab, weight = index[0], index[1]
    slabs, weights = sizes
    root = HD ** (-0.5)
    binary = root * math.log2(math.e)
    slab_inside = (slab > 0) & (slab < slabs - 1)
    weight_inside = (weight > 0) & (weight < weights - 1)
    blocks = [own, even, odd]
    blocks += [slab_even.at[i] for i in range(3)] + [slab_odd.at[i] for i in range(3)]
    outs = [parts.at[i] for parts in (parts_own, parts_even, parts_odd) for i in range(3)]
    query, cotangent = q_ref[...], co_ref[...]
    highest = None
    for j, block in enumerate(blocks):
        part = dot(query, block[:, :HD], ((1,), (1,)))
        present = None
        if j % 3 == 2:
            present = weight_inside
        if j >= 6:
            present = slab_inside if present is None else present & slab_inside
        if present is not None:
            part = part + jnp.where(present, 0.0, -jnp.inf)
        scores[j] = part
        highest = part if highest is None else jnp.maximum(highest, part)
    highest = jnp.max(highest, axis=1, keepdims=True) * binary
    total, attended = None, None
    for j, block in enumerate(blocks):
        part = jnp.exp2(scores[j] * binary - highest)
        total = part if total is None else total + part
        half = part.astype(BF)
        scores[j] = part
        halves[j] = half
        weighted = dot(half, block[:, HD:])
        attended = weighted if attended is None else attended + weighted
    scale = 1.0 / jnp.sum(total, axis=1, keepdims=True)
    attended = (attended * scale).astype(BF)
    att_ref[...] = attended
    delta = jnp.sum(cotangent.astype(F32) * attended.astype(F32), axis=1, keepdims=True)
    turned_query = query.T
    turned_cotangent = (cotangent.astype(F32) * scale).astype(BF).T
    grad_query = None
    for j, (block, out) in enumerate(zip(blocks, outs)):
        grad = dot(cotangent, block[:, HD:], ((1,), (1,)))
        grad = (scores[j] * ((grad - delta) * scale)).astype(BF)
        step = dot(grad, block[:, :HD])
        grad_query = step if grad_query is None else grad_query + step
        out[:HD, :] = (dot(turned_query, grad) * root).astype(BF)
        out[HD:, :] = dot(turned_cotangent, halves[j]).astype(BF)
    dq_ref[...] = (grad_query * root).astype(BF)


def mixed_kernel(split, att_ref, full, out_ref):
    slabs = full.shape[0]
    width = HD // slabs
    attended = att_ref[...]
    zeros = jnp.zeros((attended.shape[0], split), BF)
    total = None
    for s in range(slabs):
        part = jnp.concatenate([zeros, attended[:, s * width : (s + 1) * width]], axis=1)
        part = dot(part, full[s], ((1,), (1,)))
        total = part if total is None else total + part
    out_ref[...] = total.astype(BF)


def weight_grads_kernel(
    steps, slabs, split, index, turned, dq, own, even, odd, att_ref,
    rows_ref, keep, send, full,
):
    slab, weight = index[0], index[1]
    parity = slab & 1
    pairs = own[...] + even[...].astype(F32) + odd[...].astype(F32)
    rows = jnp.concatenate([dq[...], pairs.astype(BF).T], axis=1)
    rows_ref[...] = rows
    attended = att_ref[...]
    width = HD // slabs
    count = rows.shape[0]
    left_zeros = jnp.zeros((count, width), BF)
    right_zeros = jnp.zeros((count, split), BF)
    left, right = [], []
    for s in range(slabs):
        left += [rows[:, s * split : (s + 1) * split], left_zeros]
        right += [right_zeros, attended[:, s * width : (s + 1) * width]]
    left, right = jnp.concatenate(left, axis=1), jnp.concatenate(right, axis=1)
    grads = dot(turned[...], jnp.concatenate([left, right], axis=0))
    lanes = split + width
    for s in range(slabs):
        full[s] = grads[:, s * lanes : (s + 1) * lanes].astype(BF)
    size = keep.shape[1]
    for target, where, odd_core in ((send, slab ^ 1, 1 - parity), (keep, slab, parity)):
        for block in range(keep.shape[0]):
            s, w = block_owner(block, steps, where, weight, odd_core)
            target[block] = full[s, pl.ds(pl.multiple_of(w * size, size), size), :]


def grad_tokens_kernel(split, rows_ref, full, out_ref):
    slabs = full.shape[0]
    rows = rows_ref[...]
    zeros = jnp.zeros((rows.shape[0], HD // slabs), BF)
    total = None
    for s in range(slabs):
        part = jnp.concatenate([rows[:, s * split : (s + 1) * split], zeros], axis=1)
        part = dot(part, full[s], ((1,), (1,)))
        total = part if total is None else total + part
    out_ref[...] = total.astype(BF)


def unpack_kernel(split, keep, got, qkv_ref, proj_ref):
    total = keep[0] + got[0].astype(F32)
    qkv_ref[...] = total[:, :split]
    proj_ref[...] = total[:, split:].T


def call(kernel, outs, args, scratch=(), scalars=0, final=False):
    make = jax.ShapeDtypeStruct if final else pltpu.VMEM
    args = [
        value if i < scalars else pltpu.with_memory_space_constraint(value, pltpu.VMEM)
        for i, value in enumerate(args)
    ]
    return pl.pallas_call(
        kernel,
        out_shape=[make(shape, kind) for shape, kind in outs],
        in_specs=[SMEM] * scalars + [VMEM] * (len(args) - scalars),
        out_specs=[VMEM] * len(outs),
        scratch_shapes=list(scratch),
        compiler_params=pltpu.CompilerParams(vmem_limit_bytes=32 << 20),
    )(*args)


def local(slabs, weights, tokens, w_qkv, w_proj, grad_out):
    steps = exchange_steps(slabs, weights)
    index = jnp.stack([lax.axis_index("slab"), lax.axis_index("weight")]).astype(jnp.int32)
    count, features = tokens.shape
    rows, split = w_qkv.shape
    lanes = split + HD // slabs

    def swap(values, pairs):
        return lax.ppermute(values, AXES, pairs)

    held = pl.pallas_call(
        pack_kernel,
        out_shape=pltpu.VMEM((1, rows, lanes), BF),
        in_specs=[pl.BlockSpec(memory_space=pltpu.HBM)] * 2,
        out_specs=VMEM,
        scratch_shapes=[
            pltpu.VMEM(w_qkv.shape, BF),
            pltpu.VMEM(w_proj.shape, BF),
            pltpu.SemaphoreType.DMA((2,)),
        ],
        compiler_params=pltpu.CompilerParams(vmem_limit_bytes=32 << 20),
    )(*(pltpu.with_memory_space_constraint(value, pltpu.HBM) for value in (w_qkv, w_proj)))
    (turned,) = call(turn_kernel, [((features, 2 * count), BF)], [tokens, grad_out])
    for step in steps:
        held = jnp.concatenate([held, swap(held, step_pairs(step, slabs, weights))], axis=0)
    got = swap(held, core_pairs(slabs, weights))
    query, key_value, cotangent, full = call(
        functools.partial(project_kernel, steps, split),
        [((count, HD), BF), ((count, 2 * HD), BF), ((count, HD), BF), ((slabs, features, lanes), BF)],
        [index, held, got, tokens, grad_out],
        scalars=1,
    )

    weight_even, weight_odd = (weight_pairs(odd, slabs, weights) for odd in (0, 1))
    slab_even, slab_odd = (slab_pairs(odd, slabs, weights) for odd in (0, 1))
    even, odd = swap(key_value, weight_even), swap(key_value, weight_odd)
    even, odd, turned = lax.optimization_barrier((even, odd, turned))
    columns = jnp.stack([key_value, even, odd])
    across_even, across_odd = swap(columns, slab_even), swap(columns, slab_odd)
    pair = (3, count, 2 * HD)
    attended, grad_query, parts_own, parts_even, parts_odd = call(
        functools.partial(attention_kernel, (slabs, weights)),
        [((count, HD), BF), ((count, HD), BF), (pair, BF), (pair, BF), (pair, BF)],
        [index, query, cotangent, key_value, even, odd, across_even, across_odd],
        scratch=[pltpu.VMEM((9, count, count), F32), pltpu.VMEM((9, count, count), BF)],
        scalars=1,
    )
    parts_even, parts_odd = swap(parts_even, slab_even), swap(parts_odd, slab_odd)
    (mixed,) = call(
        functools.partial(mixed_kernel, split),
        [((count, features), BF)],
        [attended, full],
        final=True,
    )
    parts_even, parts_odd, mixed = lax.optimization_barrier((parts_even, parts_odd, mixed))

    def summed(column):
        return (
            parts_own[column].astype(F32)
            + parts_even[column].astype(F32)
            + parts_odd[column].astype(F32)
        )

    even = swap(summed(1).astype(BF), weight_even)
    odd = swap(summed(2).astype(BF), weight_odd)
    half = (1 << len(steps), rows, lanes)
    grad_rows, keep, send = call(
        functools.partial(weight_grads_kernel, steps, slabs, split),
        [((count, 3 * HD), BF), (half, BF), (half, BF)],
        [index, turned, grad_query, summed(0), even, odd, attended],
        scratch=[pltpu.VMEM((slabs, features, lanes), BF)],
        scalars=1,
    )
    got = swap(send, core_pairs(slabs, weights))
    for step in reversed(steps):
        near = keep.shape[0] // 2
        send = (keep[near:].astype(F32) + got[near:].astype(F32)).astype(BF)
        keep = keep[:near].astype(F32) + got[:near].astype(F32)
        got = swap(send, step_pairs(step, slabs, weights))
        if step == steps[-1]:
            (grad_tokens,) = call(
                functools.partial(grad_tokens_kernel, split),
                [((count, features), BF)],
                [grad_rows, full],
                final=True,
            )
            got, grad_tokens = lax.optimization_barrier((got, grad_tokens))
    grad_qkv, grad_proj = call(
        functools.partial(unpack_kernel, split),
        [((rows, split), F32), ((HD // slabs, rows), F32)],
        [keep, got],
        final=True,
    )
    return mixed, grad_tokens, grad_qkv, grad_proj


def solution(mesh):
    in_specs = (
        P(AXES, None),
        P("weight", "slab"),
        P("slab", "weight"),
        P(AXES, None),
    )
    out_specs = (
        P(AXES, None),
        P(AXES, None),
        P("weight", "slab"),
        P("slab", "weight"),
    )
    body = functools.partial(local, mesh.shape["slab"], mesh.shape["weight"])
    return jax.shard_map(body, mesh=mesh, in_specs=in_specs, out_specs=out_specs, check_vma=False)
```

```python
import functools
import math

import jax
import jax.numpy as jnp
from jax import lax
from jax.experimental import pallas as pl
from jax.experimental.pallas import tpu as pltpu
from jax.sharding import PartitionSpec as P

HD = 128
AXES = ("slab", "weight")
BF = jnp.bfloat16
F32 = jnp.float32
VMEM = pl.BlockSpec(memory_space=pltpu.VMEM)
SMEM = pl.BlockSpec(memory_space=pltpu.SMEM)


def bits_of(size):
    return size.bit_length() - 1


def exchange_steps(slabs, weights):
    steps = [((0, 1 << bit),) * 2 for bit in reversed(range(2, bits_of(weights)))]
    steps += [((1 << bit, 0),) * 2 for bit in reversed(range(2, bits_of(slabs)))]
    first, second, third = (2, 0), (0, 1), (0, 2)
    return steps + [(first, second), (second, third), (third, first)]


def block_owner(block, steps, slab, weight, odd):
    for place, (even_mask, odd_mask) in enumerate(steps):
        if block >> place & 1:
            slab = slab ^ (even_mask[0] * (1 - odd) + odd_mask[0] * odd)
            weight = weight ^ (even_mask[1] * (1 - odd) + odd_mask[1] * odd)
    return slab, weight


def step_pairs(step, slabs, weights):
    pairs = []
    for s in range(slabs):
        for w in range(weights):
            slab_mask, weight_mask = step[s & 1]
            pairs.append((s * weights + w, (s ^ slab_mask) * weights + (w ^ weight_mask)))
    return pairs


def core_pairs(slabs, weights):
    return [(s * weights + w, (s ^ 1) * weights + w) for s in range(slabs) for w in range(weights)]


def paired(index, size, odd):
    other = ((index + odd) ^ 1) - odd
    return other if 0 <= other < size else None


def slab_pairs(odd, slabs, weights):
    return [
        (s * weights + w, paired(s, slabs, odd) * weights + w)
        for s in range(slabs)
        for w in range(weights)
        if paired(s, slabs, odd) is not None
    ]


def weight_pairs(odd, slabs, weights):
    return [
        (s * weights + w, s * weights + paired(w, weights, odd))
        for s in range(slabs)
        for w in range(weights)
        if paired(w, weights, odd) is not None
    ]


def dot(a, b, dims=((1,), (0,))):
    return lax.dot_general(a, b, (dims, ((), ())), preferred_element_type=F32)


def pack_kernel(qkv_hbm, proj_hbm, out_ref, qkv_ref, proj_ref, arrived):
    first = pltpu.make_async_copy(qkv_hbm, qkv_ref, arrived.at[0])
    second = pltpu.make_async_copy(proj_hbm, proj_ref, arrived.at[1])
    first.start()
    second.start()
    first.wait()
    second.wait()
    out_ref[0] = jnp.concatenate([qkv_ref[...], proj_ref[...].T], axis=1)


def turn_kernel(tokens, grad_out, out_ref):
    count = tokens.shape[0]
    out_ref[:, :count] = tokens[...].T
    out_ref[:, count:] = grad_out[...].T


def key_value_kernel(steps, split, index, own, got, tokens, kv_ref, qkv_ref, proj_ref, full):
    slab, weight = index[0], index[1]
    odd = slab & 1
    rows = own.shape[1]
    for source, where, parity in ((own, slab, odd), (got, slab ^ 1, 1 - odd)):
        for block in range(own.shape[0]):
            s, w = block_owner(block, steps, where, weight, parity)
            full[s, pl.ds(pl.multiple_of(w * rows, rows), rows), :] = source[block]
    slabs = full.shape[0]
    qkv_ref[...] = jnp.concatenate([full[s][:, :split] for s in range(slabs)], axis=1)
    proj_ref[...] = jnp.concatenate([full[s][:, split:] for s in range(slabs)], axis=1)
    kv_ref[...] = dot(tokens[...], qkv_ref[:, HD:]).astype(BF)


def query_kernel(tokens, grad_out, qkv_ref, proj_ref, q_ref, co_ref):
    q_ref[...] = dot(tokens[...], qkv_ref[:, :HD]).astype(BF)
    co_ref[...] = dot(grad_out[...], proj_ref[...]).astype(BF)


def attention_kernel(
    sizes, index, q_ref, co_ref, own, even, odd, slab_even, slab_odd,
    att_ref, dq_ref, parts_own, parts_even, parts_odd, scores, halves,
):
    slab, weight = index[0], index[1]
    slabs, weights = sizes
    root = HD ** (-0.5)
    binary = root * math.log2(math.e)
    slab_inside = (slab > 0) & (slab < slabs - 1)
    weight_inside = (weight > 0) & (weight < weights - 1)
    blocks = [own, even, odd]
    blocks += [slab_even.at[i] for i in range(3)] + [slab_odd.at[i] for i in range(3)]
    outs = [parts.at[i] for parts in (parts_own, parts_even, parts_odd) for i in range(3)]
    query, cotangent = q_ref[...], co_ref[...]
    highest = None
    for j, block in enumerate(blocks):
        part = dot(query, block[:, :HD], ((1,), (1,)))
        present = None
        if j % 3 == 2:
            present = weight_inside
        if j >= 6:
            present = slab_inside if present is None else present & slab_inside
        if present is not None:
            part = part + jnp.where(present, 0.0, -jnp.inf)
        scores[j] = part
        highest = part if highest is None else jnp.maximum(highest, part)
    highest = jnp.max(highest, axis=1, keepdims=True) * binary
    total, attended = None, None
    for j, block in enumerate(blocks):
        part = jnp.exp2(scores[j] * binary - highest)
        total = part if total is None else total + part
        half = part.astype(BF)
        scores[j] = part
        halves[j] = half
        weighted = dot(half, block[:, HD:])
        attended = weighted if attended is None else attended + weighted
    scale = 1.0 / jnp.sum(total, axis=1, keepdims=True)
    attended = (attended * scale).astype(BF)
    att_ref[...] = attended
    delta = jnp.sum(cotangent.astype(F32) * attended.astype(F32), axis=1, keepdims=True)
    turned_query = query.T
    turned_cotangent = (cotangent.astype(F32) * scale).astype(BF).T
    grad_query = None
    for j, (block, out) in enumerate(zip(blocks, outs)):
        grad = dot(cotangent, block[:, HD:], ((1,), (1,)))
        grad = (scores[j] * ((grad - delta) * scale)).astype(BF)
        step = dot(grad, block[:, :HD])
        grad_query = step if grad_query is None else grad_query + step
        out[:HD, :] = (dot(turned_query, grad) * root).astype(BF)
        out[HD:, :] = dot(turned_cotangent, halves[j]).astype(BF)
    dq_ref[...] = (grad_query * root).astype(BF)


def mixed_kernel(att_ref, proj_ref, out_ref):
    out_ref[...] = dot(att_ref[...], proj_ref[...], ((1,), (1,))).astype(BF)


def weight_grads_kernel(
    steps, slabs, split, index, turned, dq, own, even, odd, att_ref,
    rows_ref, keep, send, full,
):
    slab, weight = index[0], index[1]
    parity = slab & 1
    pairs = own[...] + even[...].astype(F32) + odd[...].astype(F32)
    rows = jnp.concatenate([dq[...], pairs.astype(BF).T], axis=1)
    rows_ref[...] = rows
    attended = att_ref[...]
    width = HD // slabs
    count = rows.shape[0]
    left_zeros = jnp.zeros((count, width), BF)
    right_zeros = jnp.zeros((count, split), BF)
    left, right = [], []
    for s in range(slabs):
        left += [rows[:, s * split : (s + 1) * split], left_zeros]
        right += [right_zeros, attended[:, s * width : (s + 1) * width]]
    left, right = jnp.concatenate(left, axis=1), jnp.concatenate(right, axis=1)
    grads = dot(turned[...], jnp.concatenate([left, right], axis=0))
    lanes = split + width
    for s in range(slabs):
        full[s] = grads[:, s * lanes : (s + 1) * lanes].astype(BF)
    size = keep.shape[1]
    for target, where, odd_core in ((send, slab ^ 1, 1 - parity), (keep, slab, parity)):
        for block in range(keep.shape[0]):
            s, w = block_owner(block, steps, where, weight, odd_core)
            target[block] = full[s, pl.ds(pl.multiple_of(w * size, size), size), :]


def grad_tokens_kernel(rows_ref, qkv_ref, out_ref):
    out_ref[...] = dot(rows_ref[...], qkv_ref[...], ((1,), (1,))).astype(BF)


def unpack_kernel(split, keep, got, qkv_ref, proj_ref):
    total = keep[0] + got[0].astype(F32)
    qkv_ref[...] = total[:, :split]
    proj_ref[...] = total[:, split:].T


def call(kernel, outs, args, scratch=(), scalars=0, final=False):
    make = jax.ShapeDtypeStruct if final else pltpu.VMEM
    args = [
        value if i < scalars else pltpu.with_memory_space_constraint(value, pltpu.VMEM)
        for i, value in enumerate(args)
    ]
    return pl.pallas_call(
        kernel,
        out_shape=[make(shape, kind) for shape, kind in outs],
        in_specs=[SMEM] * scalars + [VMEM] * (len(args) - scalars),
        out_specs=[VMEM] * len(outs),
        scratch_shapes=list(scratch),
        compiler_params=pltpu.CompilerParams(vmem_limit_bytes=32 << 20),
    )(*args)


def local(slabs, weights, tokens, w_qkv, w_proj, grad_out):
    steps = exchange_steps(slabs, weights)
    index = jnp.stack([lax.axis_index("slab"), lax.axis_index("weight")]).astype(jnp.int32)
    count, features = tokens.shape
    rows, split = w_qkv.shape
    lanes = split + HD // slabs

    def swap(values, pairs):
        return lax.ppermute(values, AXES, pairs)

    held = pl.pallas_call(
        pack_kernel,
        out_shape=pltpu.VMEM((1, rows, lanes), BF),
        in_specs=[pl.BlockSpec(memory_space=pltpu.HBM)] * 2,
        out_specs=VMEM,
        scratch_shapes=[
            pltpu.VMEM(w_qkv.shape, BF),
            pltpu.VMEM(w_proj.shape, BF),
            pltpu.SemaphoreType.DMA((2,)),
        ],
        compiler_params=pltpu.CompilerParams(vmem_limit_bytes=32 << 20),
    )(*(pltpu.with_memory_space_constraint(value, pltpu.HBM) for value in (w_qkv, w_proj)))
    (turned,) = call(turn_kernel, [((features, 2 * count), BF)], [tokens, grad_out])
    for step in steps:
        held = jnp.concatenate([held, swap(held, step_pairs(step, slabs, weights))], axis=0)
    got = swap(held, core_pairs(slabs, weights))
    key_value, full_qkv, full_proj = call(
        functools.partial(key_value_kernel, steps, split),
        [((count, 2 * HD), BF), ((features, 3 * HD), BF), ((features, HD), BF)],
        [index, held, got, tokens],
        scratch=[pltpu.VMEM((slabs, features, lanes), BF)],
        scalars=1,
    )

    weight_even, weight_odd = (weight_pairs(odd, slabs, weights) for odd in (0, 1))
    slab_even, slab_odd = (slab_pairs(odd, slabs, weights) for odd in (0, 1))
    even, odd = swap(key_value, weight_even), swap(key_value, weight_odd)
    query, cotangent = call(
        query_kernel,
        [((count, HD), BF), ((count, HD), BF)],
        [tokens, grad_out, full_qkv, full_proj],
    )
    even, odd, turned, query, cotangent = lax.optimization_barrier(
        (even, odd, turned, query, cotangent)
    )
    columns = jnp.stack([key_value, even, odd])
    across_even, across_odd = swap(columns, slab_even), swap(columns, slab_odd)
    pair = (3, count, 2 * HD)
    attended, grad_query, parts_own, parts_even, parts_odd = call(
        functools.partial(attention_kernel, (slabs, weights)),
        [((count, HD), BF), ((count, HD), BF), (pair, BF), (pair, BF), (pair, BF)],
        [index, query, cotangent, key_value, even, odd, across_even, across_odd],
        scratch=[pltpu.VMEM((9, count, count), F32), pltpu.VMEM((9, count, count), BF)],
        scalars=1,
    )
    parts_even, parts_odd = swap(parts_even, slab_even), swap(parts_odd, slab_odd)
    (mixed,) = call(
        mixed_kernel,
        [((count, features), BF)],
        [attended, full_proj],
        final=True,
    )
    parts_even, parts_odd, mixed = lax.optimization_barrier((parts_even, parts_odd, mixed))

    def summed(column):
        return (
            parts_own[column].astype(F32)
            + parts_even[column].astype(F32)
            + parts_odd[column].astype(F32)
        )

    even = swap(summed(1).astype(BF), weight_even)
    odd = swap(summed(2).astype(BF), weight_odd)
    half = (1 << len(steps), rows, lanes)
    grad_rows, keep, send = call(
        functools.partial(weight_grads_kernel, steps, slabs, split),
        [((count, 3 * HD), BF), (half, BF), (half, BF)],
        [index, turned, grad_query, summed(0), even, odd, attended],
        scratch=[pltpu.VMEM((slabs, features, lanes), BF)],
        scalars=1,
    )
    got = swap(send, core_pairs(slabs, weights))
    for step in reversed(steps):
        near = keep.shape[0] // 2
        send = (keep[near:].astype(F32) + got[near:].astype(F32)).astype(BF)
        keep = keep[:near].astype(F32) + got[:near].astype(F32)
        got = swap(send, step_pairs(step, slabs, weights))
        if step == steps[-1]:
            (grad_tokens,) = call(
                grad_tokens_kernel,
                [((count, features), BF)],
                [grad_rows, full_qkv],
                final=True,
            )
            got, grad_tokens = lax.optimization_barrier((got, grad_tokens))
    grad_qkv, grad_proj = call(
        functools.partial(unpack_kernel, split),
        [((rows, split), F32), ((HD // slabs, rows), F32)],
        [keep, got],
        final=True,
    )
    return mixed, grad_tokens, grad_qkv, grad_proj


def solution(mesh):
    in_specs = (
        P(AXES, None),
        P("weight", "slab"),
        P("slab", "weight"),
        P(AXES, None),
    )
    out_specs = (
        P(AXES, None),
        P(AXES, None),
        P("weight", "slab"),
        P("slab", "weight"),
    )
    body = functools.partial(local, mesh.shape["slab"], mesh.shape["weight"])
    return jax.shard_map(body, mesh=mesh, in_specs=in_specs, out_specs=out_specs, check_vma=False)
```

```python
import functools
import math

import jax
import jax.numpy as jnp
from jax import lax
from jax.experimental import pallas as pl
from jax.experimental.pallas import tpu as pltpu
from jax.sharding import PartitionSpec as P

HD = 128
AXES = ("slab", "weight")
BF = jnp.bfloat16
F32 = jnp.float32
VMEM = pl.BlockSpec(memory_space=pltpu.VMEM)
SMEM = pl.BlockSpec(memory_space=pltpu.SMEM)


def bits_of(size):
    return size.bit_length() - 1


def exchange_steps(slabs, weights):
    steps = [((0, 1 << bit),) * 2 for bit in reversed(range(2, bits_of(weights)))]
    steps += [((1 << bit, 0),) * 2 for bit in reversed(range(2, bits_of(slabs)))]
    first, second, third = (2, 0), (0, 1), (0, 2)
    return steps + [(first, second), (second, third), (third, first)]


def block_owner(block, steps, slab, weight, odd):
    for place, (even_mask, odd_mask) in enumerate(steps):
        if block >> place & 1:
            slab = slab ^ (even_mask[0] * (1 - odd) + odd_mask[0] * odd)
            weight = weight ^ (even_mask[1] * (1 - odd) + odd_mask[1] * odd)
    return slab, weight


def step_pairs(step, slabs, weights):
    pairs = []
    for s in range(slabs):
        for w in range(weights):
            slab_mask, weight_mask = step[s & 1]
            pairs.append((s * weights + w, (s ^ slab_mask) * weights + (w ^ weight_mask)))
    return pairs


def core_pairs(slabs, weights):
    return [(s * weights + w, (s ^ 1) * weights + w) for s in range(slabs) for w in range(weights)]


def paired(index, size, odd):
    other = ((index + odd) ^ 1) - odd
    return other if 0 <= other < size else None


def slab_pairs(odd, slabs, weights):
    return [
        (s * weights + w, paired(s, slabs, odd) * weights + w)
        for s in range(slabs)
        for w in range(weights)
        if paired(s, slabs, odd) is not None
    ]


def weight_pairs(odd, slabs, weights):
    return [
        (s * weights + w, s * weights + paired(w, weights, odd))
        for s in range(slabs)
        for w in range(weights)
        if paired(w, weights, odd) is not None
    ]


def dot(a, b, dims=((1,), (0,))):
    return lax.dot_general(a, b, (dims, ((), ())), preferred_element_type=F32)


def pack_kernel(qkv_hbm, proj_hbm, out_ref, qkv_ref, proj_ref, arrived):
    first = pltpu.make_async_copy(qkv_hbm, qkv_ref, arrived.at[0])
    second = pltpu.make_async_copy(proj_hbm, proj_ref, arrived.at[1])
    first.start()
    second.start()
    first.wait()
    second.wait()
    out_ref[0] = jnp.concatenate([qkv_ref[...], proj_ref[...].T], axis=1)


def turn_kernel(tokens, grad_out, out_ref):
    count = tokens.shape[0]
    out_ref[:, :count] = tokens[...].T
    out_ref[:, count:] = grad_out[...].T


def key_value_kernel(steps, split, index, own, got, tokens, kv_ref, qkv_ref, proj_ref, full):
    slab, weight = index[0], index[1]
    odd = slab & 1
    rows = own.shape[1]
    for source, where, parity in ((own, slab, odd), (got, slab ^ 1, 1 - odd)):
        for block in range(own.shape[0]):
            s, w = block_owner(block, steps, where, weight, parity)
            full[s, pl.ds(pl.multiple_of(w * rows, rows), rows), :] = source[block]
    slabs = full.shape[0]
    qkv_ref[...] = jnp.concatenate([full[s][:, :split] for s in range(slabs)], axis=1)
    proj_ref[...] = jnp.concatenate([full[s][:, split:] for s in range(slabs)], axis=1)
    kv_ref[...] = dot(tokens[...], qkv_ref[:, HD:]).astype(BF)


def query_kernel(tokens, grad_out, qkv_ref, proj_ref, q_ref, co_ref):
    q_ref[...] = dot(tokens[...], qkv_ref[:, :HD]).astype(BF)
    co_ref[...] = dot(grad_out[...], proj_ref[...]).astype(BF)


def block_grads(refs, delta, scale, scores, halves, blocks, outs, total):
    query, cotangent = (ref[...] for ref in refs)
    turned_query = query.T
    turned_cotangent = (cotangent.astype(F32) * scale).astype(BF).T
    for j, (block, out) in enumerate(zip(blocks, outs)):
        grad = dot(cotangent, block[:, HD:], ((1,), (1,)))
        grad = (scores[j] * ((grad - delta) * scale)).astype(BF)
        step = dot(grad, block[:, :HD])
        total = step if total is None else total + step
        out[:HD, :] = (dot(turned_query, grad) * HD ** (-0.5)).astype(BF)
        out[HD:, :] = dot(turned_cotangent, halves[j]).astype(BF)
    return total


def attention_kernel(
    sizes, index, q_ref, co_ref, own, even, odd, side_even, side_odd, far_even, far_odd,
    att_ref, delta_ref, scale_ref, dq_ref, parts_even, parts_odd, near_scores, near_halves,
    side_scores, side_halves, scores, halves,
):
    slab, weight = index[0], index[1]
    slabs, weights = sizes
    binary = HD ** (-0.5) * math.log2(math.e)
    slab_inside = (slab > 0) & (slab < slabs - 1)
    weight_inside = (weight > 0) & (weight < weights - 1)
    far = [far_even.at[0], far_even.at[1], far_odd.at[0], far_odd.at[1]]
    blocks = far + [own, even, odd, side_even, side_odd]
    inside = [None, weight_inside, slab_inside, slab_inside & weight_inside]
    inside += [None, None, weight_inside, None, slab_inside]
    groups = ((scores, halves, 4), (near_scores, near_halves, 3), (side_scores, side_halves, 2))
    kept = [ref.at[i] for ref, _, size in groups for i in range(size)]
    kept_halves = [ref.at[i] for _, ref, size in groups for i in range(size)]
    query = q_ref[...]
    highest = None
    for block, present, place in zip(blocks, inside, kept):
        part = dot(query, block[:, :HD], ((1,), (1,)))
        if present is not None:
            part = part + jnp.where(present, 0.0, -jnp.inf)
        place[...] = part
        highest = part if highest is None else jnp.maximum(highest, part)
    highest = jnp.max(highest, axis=1, keepdims=True) * binary
    total, attended = None, None
    for block, place, half_place in zip(blocks, kept, kept_halves):
        part = jnp.exp2(place[...] * binary - highest)
        total = part if total is None else total + part
        half = part.astype(BF)
        place[...] = part
        half_place[...] = half
        weighted = dot(half, block[:, HD:])
        attended = weighted if attended is None else attended + weighted
    scale = 1.0 / jnp.sum(total, axis=1, keepdims=True)
    attended = (attended * scale).astype(BF)
    att_ref[...] = attended
    cotangent = co_ref[...].astype(F32)
    delta = jnp.sum(cotangent * attended.astype(F32), axis=1, keepdims=True)
    delta_ref[...] = delta
    scale_ref[...] = scale
    outs = [parts_even.at[0], parts_even.at[1], parts_odd.at[0], parts_odd.at[1]]
    dq_ref[...] = block_grads((q_ref, co_ref), delta, scale, scores, halves, far, outs, None)


def near_grads_kernel(
    q_ref, co_ref, own, even, odd, delta, scale, dq_part, scores, halves, dq_ref, parts,
):
    outs = [parts.at[i] for i in range(3)]
    dq_ref[...] = block_grads(
        (q_ref, co_ref), delta[...], scale[...], scores, halves, [own, even, odd], outs, dq_part[...]
    )


def side_grads_kernel(
    q_ref, co_ref, even, odd, delta, scale, dq_part, scores, halves, dq_ref, part_even, part_odd,
):
    outs = [part_even, part_odd]
    total = block_grads(
        (q_ref, co_ref), delta[...], scale[...], scores, halves, [even, odd], outs, dq_part[...]
    )
    dq_ref[...] = (total * HD ** (-0.5)).astype(BF)


def mixed_kernel(att_ref, proj_ref, out_ref):
    out_ref[...] = dot(att_ref[...], proj_ref[...], ((1,), (1,))).astype(BF)


def half_grads(steps, index, away, turned, factors, target, full):
    slab, weight = index[0], index[1]
    lanes = target.shape[2]
    grads = dot(turned[...], factors[...])
    for i in range(full.shape[0]):
        full[i] = grads[:, i * lanes : (i + 1) * lanes].astype(BF)
    size = target.shape[1]
    parity = slab & 1
    parity = 1 - parity if away else parity
    for block in range(target.shape[0]):
        s, w = block_owner(block, steps, slab ^ away, weight, parity)
        target[block] = full[s >> 1, pl.ds(pl.multiple_of(w * size, size), size), :]


def away_grads_kernel(
    steps, slabs, split, index, turned, even, odd, dq, own, side_even, side_odd, att_ref,
    rows_ref, kept, send, sent, full,
):
    pairs = own[0].astype(F32) + side_even[...].astype(F32) + side_odd[...].astype(F32)
    pairs = pairs + even[...].astype(F32) + odd[...].astype(F32)
    rows = jnp.concatenate([dq[...], pairs.astype(BF).T], axis=1)
    rows_ref[...] = rows
    attended = att_ref[...]
    width = HD // slabs
    count = rows.shape[0]
    left_zeros = jnp.zeros((count, width), BF)
    right_zeros = jnp.zeros((count, split), BF)
    halves = []
    for first in range(2):
        left, right = [], []
        for s in range(first, slabs, 2):
            left += [rows[:, s * split : (s + 1) * split], left_zeros]
            right += [right_zeros, attended[:, s * width : (s + 1) * width]]
        left, right = jnp.concatenate(left, axis=1), jnp.concatenate(right, axis=1)
        halves.append(jnp.concatenate([left, right], axis=0))
    parity = index[0] & 1

    @pl.when(parity == 0)
    def _():
        kept[...], sent[...] = halves[0], halves[1]

    @pl.when(parity == 1)
    def _():
        kept[...], sent[...] = halves[1], halves[0]

    half_grads(steps, index, 1, turned, sent, send, full)


def kept_grads_kernel(steps, index, turned, kept, keep, full):
    half_grads(steps, index, 0, turned, kept, keep, full)


def grad_tokens_kernel(rows_ref, qkv_ref, out_ref):
    out_ref[...] = dot(rows_ref[...], qkv_ref[...], ((1,), (1,))).astype(BF)


def unpack_kernel(split, keep, got, qkv_ref, proj_ref):
    total = keep[0] + got[0].astype(F32)
    qkv_ref[...] = total[:, :split]
    proj_ref[...] = total[:, split:].T


def call(kernel, outs, args, scratch=(), scalars=0, final=False):
    make = jax.ShapeDtypeStruct if final else pltpu.VMEM
    args = [
        value if i < scalars else pltpu.with_memory_space_constraint(value, pltpu.VMEM)
        for i, value in enumerate(args)
    ]
    return pl.pallas_call(
        kernel,
        out_shape=[make(shape, kind) for shape, kind in outs],
        in_specs=[SMEM] * scalars + [VMEM] * (len(args) - scalars),
        out_specs=[VMEM] * len(outs),
        scratch_shapes=list(scratch),
        compiler_params=pltpu.CompilerParams(vmem_limit_bytes=32 << 20),
    )(*args)


def local(slabs, weights, tokens, w_qkv, w_proj, grad_out):
    steps = exchange_steps(slabs, weights)
    index = jnp.stack([lax.axis_index("slab"), lax.axis_index("weight")]).astype(jnp.int32)
    count, features = tokens.shape
    rows, split = w_qkv.shape
    lanes = split + HD // slabs

    def swap(values, pairs):
        return lax.ppermute(values, AXES, pairs)

    held = pl.pallas_call(
        pack_kernel,
        out_shape=pltpu.VMEM((1, rows, lanes), BF),
        in_specs=[pl.BlockSpec(memory_space=pltpu.HBM)] * 2,
        out_specs=VMEM,
        scratch_shapes=[
            pltpu.VMEM(w_qkv.shape, BF),
            pltpu.VMEM(w_proj.shape, BF),
            pltpu.SemaphoreType.DMA((2,)),
        ],
        compiler_params=pltpu.CompilerParams(vmem_limit_bytes=32 << 20),
    )(*(pltpu.with_memory_space_constraint(value, pltpu.HBM) for value in (w_qkv, w_proj)))
    (turned,) = call(turn_kernel, [((features, 2 * count), BF)], [tokens, grad_out])
    for step in steps:
        held = jnp.concatenate([held, swap(held, step_pairs(step, slabs, weights))], axis=0)
    got = swap(held, core_pairs(slabs, weights))
    key_value, full_qkv, full_proj = call(
        functools.partial(key_value_kernel, steps, split),
        [((count, 2 * HD), BF), ((features, 3 * HD), BF), ((features, HD), BF)],
        [index, held, got, tokens],
        scratch=[pltpu.VMEM((slabs, features, lanes), BF)],
        scalars=1,
    )

    weight_even, weight_odd = (weight_pairs(odd, slabs, weights) for odd in (0, 1))
    slab_even, slab_odd = (slab_pairs(odd, slabs, weights) for odd in (0, 1))
    side_even, side_odd = swap(key_value, slab_even), swap(key_value, slab_odd)
    even, odd = swap(key_value, weight_even), swap(key_value, weight_odd)
    query, cotangent = call(
        query_kernel,
        [((count, HD), BF), ((count, HD), BF)],
        [tokens, grad_out, full_qkv, full_proj],
    )
    side_even, side_odd, even, odd, turned, query, cotangent = lax.optimization_barrier(
        (side_even, side_odd, even, odd, turned, query, cotangent)
    )
    columns = jnp.stack([even, odd])
    far_even, far_odd = swap(columns, slab_even), swap(columns, slab_odd)
    one = (count, 2 * HD)
    square = (count, count)
    (
        attended, delta, scale, grad_query, parts_even, parts_odd,
        scores, halves, side_scores, side_halves,
    ) = call(
        functools.partial(attention_kernel, (slabs, weights)),
        [
            ((count, HD), BF), ((count, 1), F32), ((count, 1), F32), ((count, HD), F32),
            ((2, *one), BF), ((2, *one), BF), ((3, *square), F32), ((3, *square), BF),
            ((2, *square), F32), ((2, *square), BF),
        ],
        [
            index, query, cotangent, key_value, even, odd,
            side_even, side_odd, far_even, far_odd,
        ],
        scratch=[pltpu.VMEM((4, *square), F32), pltpu.VMEM((4, *square), BF)],
        scalars=1,
    )
    parts_even, parts_odd = swap(parts_even, slab_even), swap(parts_odd, slab_odd)
    grad_query, parts_own = call(
        near_grads_kernel,
        [((count, HD), F32), ((3, *one), BF)],
        [query, cotangent, key_value, even, odd, delta, scale, grad_query, scores, halves],
    )
    (mixed,) = call(
        mixed_kernel,
        [((count, features), BF)],
        [attended, full_proj],
        final=True,
    )
    parts_even, parts_odd, parts_own, mixed = lax.optimization_barrier(
        (parts_even, parts_odd, parts_own, mixed)
    )

    def summed(column):
        total = parts_own[column + 1].astype(F32)
        total = total + parts_even[column].astype(F32) + parts_odd[column].astype(F32)
        return total.astype(BF)

    grad_query, even, odd = lax.optimization_barrier((grad_query, summed(0), summed(1)))
    grad_query, side_even, side_odd = call(
        side_grads_kernel,
        [((count, HD), BF), (one, BF), (one, BF)],
        [
            query, cotangent, side_even, side_odd, delta, scale, grad_query,
            side_scores, side_halves,
        ],
    )
    side_even, side_odd = swap(side_even, slab_even), swap(side_odd, slab_odd)
    even, odd = swap(even, weight_even), swap(odd, weight_odd)
    half = (1 << len(steps), rows, lanes)
    factors = (2 * count, slabs // 2 * lanes)
    grad_rows, kept, send = call(
        functools.partial(away_grads_kernel, steps, slabs, split),
        [((count, 3 * HD), BF), (factors, BF), (half, BF)],
        [index, turned, even, odd, grad_query, parts_own, side_even, side_odd, attended],
        scratch=[pltpu.VMEM(factors, BF), pltpu.VMEM((slabs // 2, features, lanes), BF)],
        scalars=1,
    )
    got = swap(send, core_pairs(slabs, weights))
    (keep,) = call(
        functools.partial(kept_grads_kernel, steps),
        [(half, BF)],
        [index, turned, kept],
        scratch=[pltpu.VMEM((slabs // 2, features, lanes), BF)],
        scalars=1,
    )
    got, keep = lax.optimization_barrier((got, keep))
    for step in reversed(steps):
        near = keep.shape[0] // 2
        send = (keep[near:].astype(F32) + got[near:].astype(F32)).astype(BF)
        keep = keep[:near].astype(F32) + got[:near].astype(F32)
        got = swap(send, step_pairs(step, slabs, weights))
        if step == steps[-1]:
            (grad_tokens,) = call(
                grad_tokens_kernel,
                [((count, features), BF)],
                [grad_rows, full_qkv],
                final=True,
            )
            got, grad_tokens = lax.optimization_barrier((got, grad_tokens))
    grad_qkv, grad_proj = call(
        functools.partial(unpack_kernel, split),
        [((rows, split), F32), ((HD // slabs, rows), F32)],
        [keep, got],
        final=True,
    )
    return mixed, grad_tokens, grad_qkv, grad_proj


def solution(mesh):
    in_specs = (
        P(AXES, None),
        P("weight", "slab"),
        P("slab", "weight"),
        P(AXES, None),
    )
    out_specs = (
        P(AXES, None),
        P(AXES, None),
        P("weight", "slab"),
        P("slab", "weight"),
    )
    body = functools.partial(local, mesh.shape["slab"], mesh.shape["weight"])
    return jax.shard_map(body, mesh=mesh, in_specs=in_specs, out_specs=out_specs, check_vma=False)
```

```python
import functools
import math

import jax
import jax.numpy as jnp
from jax import lax
from jax.experimental import pallas as pl
from jax.experimental.pallas import tpu as pltpu
from jax.sharding import PartitionSpec as P

HD = 128
BINARY = HD ** (-0.5) * math.log2(math.e)
AXES = ("slab", "weight")
BF = jnp.bfloat16
F32 = jnp.float32
VMEM = pl.BlockSpec(memory_space=pltpu.VMEM)
SMEM = pl.BlockSpec(memory_space=pltpu.SMEM)


def bits_of(size):
    return size.bit_length() - 1


def exchange_steps(slabs, weights):
    steps = [((0, 1 << bit),) * 2 for bit in reversed(range(2, bits_of(weights)))]
    steps += [((1 << bit, 0),) * 2 for bit in reversed(range(2, bits_of(slabs)))]
    first, second, third = (2, 0), (0, 1), (0, 2)
    return steps + [(first, second), (second, third), (third, first)]


def block_owner(block, steps, slab, weight, odd):
    for place, (even_mask, odd_mask) in enumerate(steps):
        if block >> place & 1:
            slab = slab ^ (even_mask[0] * (1 - odd) + odd_mask[0] * odd)
            weight = weight ^ (even_mask[1] * (1 - odd) + odd_mask[1] * odd)
    return slab, weight


def step_pairs(step, slabs, weights):
    pairs = []
    for s in range(slabs):
        for w in range(weights):
            slab_mask, weight_mask = step[s & 1]
            pairs.append((s * weights + w, (s ^ slab_mask) * weights + (w ^ weight_mask)))
    return pairs


def core_pairs(slabs, weights):
    return [(s * weights + w, (s ^ 1) * weights + w) for s in range(slabs) for w in range(weights)]


def paired(index, size, odd):
    other = ((index + odd) ^ 1) - odd
    return other if 0 <= other < size else None


def slab_pairs(odd, slabs, weights):
    return [
        (s * weights + w, paired(s, slabs, odd) * weights + w)
        for s in range(slabs)
        for w in range(weights)
        if paired(s, slabs, odd) is not None
    ]


def weight_pairs(odd, slabs, weights):
    return [
        (s * weights + w, s * weights + paired(w, weights, odd))
        for s in range(slabs)
        for w in range(weights)
        if paired(w, weights, odd) is not None
    ]


def dot(a, b, dims=((1,), (0,))):
    return lax.dot_general(a, b, (dims, ((), ())), preferred_element_type=F32)


def pack_kernel(qkv_hbm, proj_hbm, out_ref, qkv_ref, proj_ref, arrived):
    first = pltpu.make_async_copy(qkv_hbm, qkv_ref, arrived.at[0])
    second = pltpu.make_async_copy(proj_hbm, proj_ref, arrived.at[1])
    first.start()
    second.start()
    first.wait()
    second.wait()
    out_ref[0] = jnp.concatenate([qkv_ref[...], proj_ref[...].T], axis=1)


def turn_kernel(tokens, grad_out, out_ref):
    count = tokens.shape[0]
    out_ref[:, :count] = tokens[...].T
    out_ref[:, count:] = grad_out[...].T


def key_value_kernel(steps, split, index, own, got, tokens, kv_ref, qkv_ref, proj_ref, full):
    slab, weight = index[0], index[1]
    odd = slab & 1
    rows = own.shape[1]
    for source, where, parity in ((own, slab, odd), (got, slab ^ 1, 1 - odd)):
        for block in range(own.shape[0]):
            s, w = block_owner(block, steps, where, weight, parity)
            full[s, pl.ds(pl.multiple_of(w * rows, rows), rows), :] = source[block]
    slabs = full.shape[0]
    qkv_ref[...] = jnp.concatenate([full[s][:, :split] for s in range(slabs)], axis=1)
    proj_ref[...] = jnp.concatenate([full[s][:, split:] for s in range(slabs)], axis=1)
    kv_ref[...] = dot(tokens[...], qkv_ref[:, HD:]).astype(BF)


def query_kernel(tokens, grad_out, qkv_ref, proj_ref, q_ref, co_ref):
    q_ref[...] = dot(tokens[...], qkv_ref[:, :HD]).astype(BF)
    co_ref[...] = dot(grad_out[...], proj_ref[...]).astype(BF)


def block_grads(refs, delta, scale, scores, halves, blocks, outs, total):
    query, cotangent = (ref[...] for ref in refs)
    turned_query = query.T
    turned_cotangent = (cotangent.astype(F32) * scale).astype(BF).T
    for j, (block, out) in enumerate(zip(blocks, outs)):
        grad = dot(cotangent, block[:, HD:], ((1,), (1,)))
        grad = (scores[j] * ((grad - delta) * scale)).astype(BF)
        step = dot(grad, block[:, :HD])
        total = step if total is None else total + step
        out[:HD, :] = (dot(turned_query, grad) * HD ** (-0.5)).astype(BF)
        out[HD:, :] = dot(turned_cotangent, halves[j]).astype(BF)
    return total


def window_scores(query, blocks, inside, kept):
    highest = None
    for block, present, place in zip(blocks, inside, kept):
        part = dot(query, block[:, :HD], ((1,), (1,)))
        if present is not None:
            part = part + jnp.where(present, 0.0, -jnp.inf)
        place[...] = part
        highest = part if highest is None else jnp.maximum(highest, part)
    return jnp.max(highest, axis=1, keepdims=True) * BINARY


def window_values(highest, blocks, kept, kept_halves):
    total, attended = None, None
    for block, place, half_place in zip(blocks, kept, kept_halves):
        part = jnp.exp2(place[...] * BINARY - highest)
        total = part if total is None else total + part
        half = part.astype(BF)
        place[...] = part
        half_place[...] = half
        weighted = dot(half, block[:, HD:])
        attended = weighted if attended is None else attended + weighted
    return jnp.sum(total, axis=1, keepdims=True), attended


def inner(index, axis, size):
    return (index[axis] > 0) & (index[axis] < size - 1)


def near_kernel(
    sizes, index, q_ref, own, even, odd, side_even, side_odd,
    high_ref, total_ref, sum_ref, near_scores, near_halves, side_scores, side_halves,
):
    blocks = [own, even, odd, side_even, side_odd]
    inside = [None, None, inner(index, 1, sizes[1]), None, inner(index, 0, sizes[0])]
    kept = [near_scores.at[i] for i in range(3)] + [side_scores.at[i] for i in range(2)]
    halves = [near_halves.at[i] for i in range(3)] + [side_halves.at[i] for i in range(2)]
    highest = window_scores(q_ref[...], blocks, inside, kept)
    high_ref[...] = highest
    total_ref[...], sum_ref[...] = window_values(highest, blocks, kept, halves)


def attention_kernel(
    sizes, index, q_ref, co_ref, far_even, far_odd, near_high, near_total, near_sum,
    att_ref, delta_ref, scale_ref, dq_ref, parts_even, parts_odd, scores, halves,
):
    slab_inside, weight_inside = inner(index, 0, sizes[0]), inner(index, 1, sizes[1])
    blocks = [far_even.at[0], far_even.at[1], far_odd.at[0], far_odd.at[1]]
    inside = [None, weight_inside, slab_inside, slab_inside & weight_inside]
    kept, kept_halves = ([ref.at[i] for i in range(4)] for ref in (scores, halves))
    highest = window_scores(q_ref[...], blocks, inside, kept)
    highest = jnp.maximum(highest, near_high[...])
    shrink = jnp.exp2(near_high[...] - highest)
    total, attended = window_values(highest, blocks, kept, kept_halves)
    scale = 1.0 / (total + near_total[...] * shrink)
    attended = ((attended + near_sum[...] * shrink) * scale).astype(BF)
    att_ref[...] = attended
    cotangent = co_ref[...].astype(F32)
    delta = jnp.sum(cotangent * attended.astype(F32), axis=1, keepdims=True)
    delta_ref[...] = delta
    scale_ref[...] = scale * shrink
    outs = [parts_even.at[0], parts_even.at[1], parts_odd.at[0], parts_odd.at[1]]
    dq_ref[...] = block_grads((q_ref, co_ref), delta, scale, scores, halves, blocks, outs, None)


def near_grads_kernel(
    q_ref, co_ref, own, even, odd, delta, scale, dq_part, scores, halves, dq_ref, parts,
):
    outs = [parts.at[i] for i in range(3)]
    dq_ref[...] = block_grads(
        (q_ref, co_ref), delta[...], scale[...], scores, halves, [own, even, odd], outs, dq_part[...]
    )


def side_grads_kernel(
    q_ref, co_ref, even, odd, delta, scale, dq_part, scores, halves, dq_ref, part_even, part_odd,
):
    outs = [part_even, part_odd]
    total = block_grads(
        (q_ref, co_ref), delta[...], scale[...], scores, halves, [even, odd], outs, dq_part[...]
    )
    dq_ref[...] = (total * HD ** (-0.5)).astype(BF)


def mixed_kernel(att_ref, proj_ref, out_ref):
    out_ref[...] = dot(att_ref[...], proj_ref[...], ((1,), (1,))).astype(BF)


def half_grads(steps, index, away, turned, factors, target, full):
    slab, weight = index[0], index[1]
    lanes = target.shape[2]
    grads = dot(turned[...], factors[...])
    for i in range(full.shape[0]):
        full[i] = grads[:, i * lanes : (i + 1) * lanes].astype(BF)
    size = target.shape[1]
    parity = slab & 1
    parity = 1 - parity if away else parity
    for block in range(target.shape[0]):
        s, w = block_owner(block, steps, slab ^ away, weight, parity)
        target[block] = full[s >> 1, pl.ds(pl.multiple_of(w * size, size), size), :]


def away_grads_kernel(
    steps, slabs, split, index, turned, even, odd, dq, own, side_even, side_odd, att_ref,
    rows_ref, kept, send, sent, full,
):
    pairs = own[0].astype(F32) + side_even[...].astype(F32) + side_odd[...].astype(F32)
    pairs = pairs + even[...].astype(F32) + odd[...].astype(F32)
    rows = jnp.concatenate([dq[...], pairs.astype(BF).T], axis=1)
    rows_ref[...] = rows
    attended = att_ref[...]
    width = HD // slabs
    count = rows.shape[0]
    left_zeros = jnp.zeros((count, width), BF)
    right_zeros = jnp.zeros((count, split), BF)
    halves = []
    for first in range(2):
        left, right = [], []
        for s in range(first, slabs, 2):
            left += [rows[:, s * split : (s + 1) * split], left_zeros]
            right += [right_zeros, attended[:, s * width : (s + 1) * width]]
        left, right = jnp.concatenate(left, axis=1), jnp.concatenate(right, axis=1)
        halves.append(jnp.concatenate([left, right], axis=0))
    parity = index[0] & 1

    @pl.when(parity == 0)
    def _():
        kept[...], sent[...] = halves[0], halves[1]

    @pl.when(parity == 1)
    def _():
        kept[...], sent[...] = halves[1], halves[0]

    half_grads(steps, index, 1, turned, sent, send, full)


def kept_grads_kernel(steps, index, turned, kept, keep, full):
    half_grads(steps, index, 0, turned, kept, keep, full)


def grad_tokens_kernel(rows_ref, qkv_ref, out_ref):
    out_ref[...] = dot(rows_ref[...], qkv_ref[...], ((1,), (1,))).astype(BF)


def unpack_kernel(split, keep, got, qkv_ref, proj_ref):
    total = keep[0] + got[0].astype(F32)
    qkv_ref[...] = total[:, :split]
    proj_ref[...] = total[:, split:].T


def call(kernel, outs, args, scratch=(), scalars=0, final=False):
    make = jax.ShapeDtypeStruct if final else pltpu.VMEM
    args = [
        value if i < scalars else pltpu.with_memory_space_constraint(value, pltpu.VMEM)
        for i, value in enumerate(args)
    ]
    return pl.pallas_call(
        kernel,
        out_shape=[make(shape, kind) for shape, kind in outs],
        in_specs=[SMEM] * scalars + [VMEM] * (len(args) - scalars),
        out_specs=[VMEM] * len(outs),
        scratch_shapes=list(scratch),
        compiler_params=pltpu.CompilerParams(vmem_limit_bytes=32 << 20),
    )(*args)


def local(slabs, weights, tokens, w_qkv, w_proj, grad_out):
    steps = exchange_steps(slabs, weights)
    index = jnp.stack([lax.axis_index("slab"), lax.axis_index("weight")]).astype(jnp.int32)
    count, features = tokens.shape
    rows, split = w_qkv.shape
    lanes = split + HD // slabs

    def swap(values, pairs):
        return lax.ppermute(values, AXES, pairs)

    held = pl.pallas_call(
        pack_kernel,
        out_shape=pltpu.VMEM((1, rows, lanes), BF),
        in_specs=[pl.BlockSpec(memory_space=pltpu.HBM)] * 2,
        out_specs=VMEM,
        scratch_shapes=[
            pltpu.VMEM(w_qkv.shape, BF),
            pltpu.VMEM(w_proj.shape, BF),
            pltpu.SemaphoreType.DMA((2,)),
        ],
        compiler_params=pltpu.CompilerParams(vmem_limit_bytes=32 << 20),
    )(*(pltpu.with_memory_space_constraint(value, pltpu.HBM) for value in (w_qkv, w_proj)))
    (turned,) = call(turn_kernel, [((features, 2 * count), BF)], [tokens, grad_out])
    for step in steps:
        held = jnp.concatenate([held, swap(held, step_pairs(step, slabs, weights))], axis=0)
    got = swap(held, core_pairs(slabs, weights))
    key_value, full_qkv, full_proj = call(
        functools.partial(key_value_kernel, steps, split),
        [((count, 2 * HD), BF), ((features, 3 * HD), BF), ((features, HD), BF)],
        [index, held, got, tokens],
        scratch=[pltpu.VMEM((slabs, features, lanes), BF)],
        scalars=1,
    )

    weight_even, weight_odd = (weight_pairs(odd, slabs, weights) for odd in (0, 1))
    slab_even, slab_odd = (slab_pairs(odd, slabs, weights) for odd in (0, 1))
    side_even, side_odd = swap(key_value, slab_even), swap(key_value, slab_odd)
    even, odd = swap(key_value, weight_even), swap(key_value, weight_odd)
    query, cotangent = call(
        query_kernel,
        [((count, HD), BF), ((count, HD), BF)],
        [tokens, grad_out, full_qkv, full_proj],
    )
    side_even, side_odd, even, odd, turned, query, cotangent = lax.optimization_barrier(
        (side_even, side_odd, even, odd, turned, query, cotangent)
    )
    columns = jnp.stack([even, odd])
    far_even, far_odd = swap(columns, slab_even), swap(columns, slab_odd)
    one = (count, 2 * HD)
    square = (count, count)
    column = (count, 1)
    high, total, partial, scores, halves, side_scores, side_halves = call(
        functools.partial(near_kernel, (slabs, weights)),
        [
            (column, F32), (column, F32), ((count, HD), F32), ((3, *square), F32),
            ((3, *square), BF), ((2, *square), F32), ((2, *square), BF),
        ],
        [index, query, key_value, even, odd, side_even, side_odd],
        scalars=1,
    )
    far_even, far_odd, partial = lax.optimization_barrier((far_even, far_odd, partial))
    attended, delta, scale, grad_query, parts_even, parts_odd = call(
        functools.partial(attention_kernel, (slabs, weights)),
        [
            ((count, HD), BF), (column, F32), (column, F32), ((count, HD), F32),
            ((2, *one), BF), ((2, *one), BF),
        ],
        [index, query, cotangent, far_even, far_odd, high, total, partial],
        scratch=[pltpu.VMEM((4, *square), F32), pltpu.VMEM((4, *square), BF)],
        scalars=1,
    )
    parts_even, parts_odd = swap(parts_even, slab_even), swap(parts_odd, slab_odd)
    grad_query, parts_own = call(
        near_grads_kernel,
        [((count, HD), F32), ((3, *one), BF)],
        [query, cotangent, key_value, even, odd, delta, scale, grad_query, scores, halves],
    )
    grad_query, side_even, side_odd = call(
        side_grads_kernel,
        [((count, HD), BF), (one, BF), (one, BF)],
        [
            query, cotangent, side_even, side_odd, delta, scale, grad_query,
            side_scores, side_halves,
        ],
    )
    side_even, side_odd = swap(side_even, slab_even), swap(side_odd, slab_odd)
    (mixed,) = call(
        mixed_kernel,
        [((count, features), BF)],
        [attended, full_proj],
        final=True,
    )
    parts_even, parts_odd, parts_own, grad_query, mixed = lax.optimization_barrier(
        (parts_even, parts_odd, parts_own, grad_query, mixed)
    )

    def summed(column):
        total = parts_own[column + 1].astype(F32)
        total = total + parts_even[column].astype(F32) + parts_odd[column].astype(F32)
        return total.astype(BF)

    even, odd = swap(summed(0), weight_even), swap(summed(1), weight_odd)
    half = (1 << len(steps), rows, lanes)
    factors = (2 * count, slabs // 2 * lanes)
    grad_rows, kept, send = call(
        functools.partial(away_grads_kernel, steps, slabs, split),
        [((count, 3 * HD), BF), (factors, BF), (half, BF)],
        [index, turned, even, odd, grad_query, parts_own, side_even, side_odd, attended],
        scratch=[pltpu.VMEM(factors, BF), pltpu.VMEM((slabs // 2, features, lanes), BF)],
        scalars=1,
    )
    got = swap(send, core_pairs(slabs, weights))
    (keep,) = call(
        functools.partial(kept_grads_kernel, steps),
        [(half, BF)],
        [index, turned, kept],
        scratch=[pltpu.VMEM((slabs // 2, features, lanes), BF)],
        scalars=1,
    )
    got, keep = lax.optimization_barrier((got, keep))
    for step in reversed(steps):
        near = keep.shape[0] // 2
        send = (keep[near:].astype(F32) + got[near:].astype(F32)).astype(BF)
        keep = keep[:near].astype(F32) + got[:near].astype(F32)
        got = swap(send, step_pairs(step, slabs, weights))
        if step == steps[-1]:
            (grad_tokens,) = call(
                grad_tokens_kernel,
                [((count, features), BF)],
                [grad_rows, full_qkv],
                final=True,
            )
            got, grad_tokens = lax.optimization_barrier((got, grad_tokens))
    grad_qkv, grad_proj = call(
        functools.partial(unpack_kernel, split),
        [((rows, split), F32), ((HD // slabs, rows), F32)],
        [keep, got],
        final=True,
    )
    return mixed, grad_tokens, grad_qkv, grad_proj


def solution(mesh):
    in_specs = (
        P(AXES, None),
        P("weight", "slab"),
        P("slab", "weight"),
        P(AXES, None),
    )
    out_specs = (
        P(AXES, None),
        P(AXES, None),
        P("weight", "slab"),
        P("slab", "weight"),
    )
    body = functools.partial(local, mesh.shape["slab"], mesh.shape["weight"])
    return jax.shard_map(body, mesh=mesh, in_specs=in_specs, out_specs=out_specs, check_vma=False)
```
